32 devices in a mesh: expert: 4 (over z), fsdp: 8 (over y, x, core).
Axes of the slice: x: 2, y: 2, z: 4, core: 2. Of those that a mesh axis runs over, the one named last changes fastest.
Arguments:
- tokens: bfloat16 [8192, 2048], P(('expert', 'fsdp')), may hold values from -6 to 6
- expert_ids: int32 [8192, 6], P(('expert', 'fsdp')), may hold values from 0 to 63, as said below
- gate_vals: bfloat16 [8192, 6], P(('expert', 'fsdp')), may hold values from 0.099609375 to 1
- w_gate: bfloat16 [4, 2048, 1408], P('expert', 'fsdp'), may hold values from -0.125 to 0.125
- w_up: bfloat16 [4, 2048, 1408], P('expert', 'fsdp'), may hold values from -0.125 to 0.125
- w_down: bfloat16 [4, 2048, 1408], P('expert', 'fsdp'), may hold values from -0.15625 to 0.15625
- cotangent: bfloat16 [8192, 2048], P(('expert', 'fsdp')), may hold values from -6 to 6
Outputs:
- output: bfloat16 [8192, 2048], P(('expert', 'fsdp'))
- grad_tokens: bfloat16 [8192, 2048], P(('expert', 'fsdp'))
- grad_gates: float32 [8192, 6], P(('expert', 'fsdp'))
- grad_w_gate: float32 [4, 2048, 1408], P('expert', 'fsdp')
- grad_w_up: float32 [4, 2048, 1408], P('expert', 'fsdp')
- grad_w_down: float32 [4, 2048, 1408], P('expert', 'fsdp')
The draws below stay inside these ranges and needn't reach their ends.
Inputs may be any that keep to these rules, and one draw needn't show every extreme that they name: `expert_ids`: each row names 6 different experts. Among the tokens of one device at most 48 name any one expert whose number modulo 16 is below 1. On every device some such expert is named by exactly 48 of its tokens, and for every column one such expert is named by exactly 48 tokens of every device of that column.
All inputs are finite; a program needn't handle non-finite values.
Results may differ from the reference program's by a relative error of at most 0.013.
Values may be sent and summed in bfloat16 or wider, within the bound.
A program may use at most 128 MiB of HBM per device.

```python
import jax
import jax.numpy as jnp
from jax import lax

D = 2048
FF = 1408
EXPERTS = 64
TOP = 6
TOK_DEV = 256
WAVE = 1
GROUPS = 4
COLUMNS = 8
PER_INDEX = 16
WINDOW = 4
MOST = 48
TOKENS = 8192


def block_routes(key, block):
    column_index = block % COLUMNS
    hot_pick = jax.random.randint(jax.random.fold_in(key, 7), (COLUMNS,), 0, WINDOW)[column_index]
    block_key = jax.random.fold_in(key, block + 11)
    key_shift, key_perm, key_score, key_order = jax.random.split(block_key, 4)
    shifts = jax.random.randint(key_shift, (WINDOW,), 0, 3)
    levels = jnp.array([MOST, MOST // 2, MOST // 4], jnp.int32)
    counts = levels[shifts]
    counts = jnp.where(jnp.arange(WINDOW) == hot_pick, MOST, counts).astype(jnp.int32)
    starts = jnp.cumsum(counts) - counts
    position = jnp.arange(TOK_DEV, dtype=jnp.int32)
    covered = (position[:, None] - starts[None, :]) % TOK_DEV < counts[None, :]
    shuffle = jax.random.permutation(key_perm, TOK_DEV)
    token_cover = covered[shuffle]
    window_ids = jnp.arange(WINDOW, dtype=jnp.int32)
    window_expert = window_ids // WAVE * PER_INDEX + window_ids % WAVE
    cover_full = jnp.zeros((TOK_DEV, EXPERTS), jnp.bool_).at[:, window_expert].set(token_cover)
    expert_range = jnp.arange(EXPERTS, dtype=jnp.int32)
    in_window = expert_range % PER_INDEX < WAVE
    base = jax.random.randint(key_score, (TOK_DEV, EXPERTS), 0, 2 ** 16) * EXPERTS + expert_range[None, :]
    chosen_score = jnp.where(cover_full, 2 ** 30 + expert_range[None, :], -1 - expert_range[None, :])
    score = jnp.where(in_window[None, :], chosen_score, base)
    unused, picks = lax.top_k(score, TOP)
    order_keys = jax.random.randint(key_order, (TOK_DEV, TOP), 0, 2 ** 16) * TOP + jnp.arange(TOP, dtype=jnp.int32)[None, :]
    slot_order = jnp.argsort(order_keys, axis=1)
    return jnp.take_along_axis(picks, slot_order, axis=1).astype(jnp.int32)


def draw_expert_ids(key, part):
    blocks = jnp.arange(GROUPS * COLUMNS, dtype=jnp.int32)
    routed = jax.vmap(lambda block: block_routes(key, block))(blocks)
    return routed.reshape(TOKENS, TOP).astype(jnp.int32)


def block_scale(rng, shape, pieces, least, largest):
    gain, own = 1.0, jax.random.fold_in(rng, 6)
    for dim, blocks in pieces:
        heights = jnp.exp(jax.random.uniform(jax.random.fold_in(own, dim), (blocks,), jnp.float32, least / len(pieces), largest / len(pieces)))
        gain = gain * jnp.repeat(heights, shape[dim] // blocks).reshape([-1 if axis == dim else 1 for axis in range(len(shape))])
    return gain


def normal_values(stream_key, dims, spread, reach, cuts=(), kind=jnp.bfloat16):
    factor_of = block_scale(stream_key, dims, cuts, -0.22, 0.18) if cuts else 1.0
    values = jax.random.normal(stream_key, dims, jnp.float32) * spread * factor_of
    return jnp.minimum(jnp.maximum(values, -reach), reach).astype(kind)


def setup_inputs(seed: int = 0) -> dict:
    arg_keys = jax.random.split(jax.random.key(seed), 8)
    tokens = normal_values(arg_keys[0], (TOKENS, D), 1.0, 6.0, ((0, 32),))
    expert_ids = draw_expert_ids(jax.random.fold_in(arg_keys[7], 71), 0)
    gate_vals = jnp.clip(0.099609375 + 0.9003906 * jax.random.uniform(arg_keys[2], (TOKENS, TOP), jnp.float32) ** block_scale(arg_keys[2], (TOKENS, TOP), ((0, 32),), -0.2, 0.2), 0.099609375, 1.0).astype(jnp.bfloat16)
    w_gate = normal_values(arg_keys[3], (WINDOW, D, FF), D ** -0.5, 0.125, ((0, 4), (1, 8)))
    w_up = normal_values(arg_keys[4], (WINDOW, D, FF), D ** -0.5, 0.125, ((0, 4), (1, 8)))
    w_down = normal_values(arg_keys[5], (WINDOW, D, FF), FF ** -0.5, 0.15625, ((0, 4), (1, 8)))
    cotangent = normal_values(arg_keys[6], (TOKENS, D), 1.0, 6.0, ((0, 32),))
    return {"tokens": tokens, "expert_ids": expert_ids, "gate_vals": gate_vals, "w_gate": w_gate, "w_up": w_up, "w_down": w_down, "cotangent": cotangent}


def reference(tokens, expert_ids, gate_vals, w_gate, w_up, w_down, cotangent):
    slot_total = TOKENS * TOP
    model_width = tokens.shape[1]
    flat_ids = expert_ids.reshape(-1).astype(jnp.int32)
    local_index = flat_ids % PER_INDEX
    is_live = local_index < WAVE
    window_slot = jnp.where(is_live, (flat_ids // PER_INDEX) * WAVE + local_index, WINDOW).astype(jnp.int32)
    slot_ids = jnp.arange(slot_total, dtype=jnp.int32)
    column = ((slot_ids // TOP) // TOK_DEV) % COLUMNS
    zero_row = jnp.zeros((1, model_width), tokens.dtype)
    tokens_pad = jnp.concatenate([tokens, zero_row], axis=0)
    cot_pad = jnp.concatenate([cotangent, zero_row], axis=0)
    gate_pad = jnp.concatenate([gate_vals.reshape(-1), jnp.zeros((1,), gate_vals.dtype)], axis=0)
    capacity = GROUPS * MOST

    def pair_step(running, column_index, expert):
        out_acc, grad_acc, gate_acc, sum_gate, sum_up, sum_down = running
        chosen = (window_slot == expert) & (column == column_index)
        picked = jnp.nonzero(chosen, size=capacity, fill_value=slot_total)[0].astype(jnp.int32)
        token_at = (picked // TOP).astype(jnp.int32)
        row_data = tokens_pad[token_at]
        cot_rows = cot_pad[token_at]
        gate_rows = gate_pad[picked].astype(jnp.float32)
        weight_gate = w_gate[expert]
        weight_up = w_up[expert]
        weight_down = w_down[expert]
        gate_pre = jnp.dot(row_data, weight_gate, preferred_element_type=jnp.float32)
        up_pre = jnp.dot(row_data, weight_up, preferred_element_type=jnp.float32)
        sigmoid_g = jax.nn.sigmoid(gate_pre)
        hidden = (gate_pre * sigmoid_g * up_pre).astype(jnp.bfloat16)
        expert_out = jnp.dot(hidden, weight_down.T, preferred_element_type=jnp.float32).astype(jnp.bfloat16)
        out_f = expert_out.astype(jnp.float32)
        out_acc = out_acc.at[token_at].add(gate_rows[:, None] * out_f, mode="drop")
        gate_acc = gate_acc.at[picked].add(jnp.sum(cot_rows.astype(jnp.float32) * out_f, axis=1), mode="drop")
        out_grad = (gate_rows[:, None] * cot_rows.astype(jnp.float32)).astype(jnp.bfloat16)
        hidden_grad = jnp.dot(out_grad, weight_down, preferred_element_type=jnp.float32)
        gate_grad = (hidden_grad * up_pre * sigmoid_g * (1.0 + gate_pre * (1.0 - sigmoid_g))).astype(jnp.bfloat16)
        up_grad = (hidden_grad * gate_pre * sigmoid_g).astype(jnp.bfloat16)
        slot_grad = (jnp.dot(gate_grad, weight_gate.T, preferred_element_type=jnp.float32)
                     + jnp.dot(up_grad, weight_up.T, preferred_element_type=jnp.float32)).astype(jnp.bfloat16)
        grad_acc = grad_acc.at[token_at].add(slot_grad.astype(jnp.float32), mode="drop")
        part_gate = jnp.dot(row_data.T, gate_grad, preferred_element_type=jnp.float32).astype(jnp.bfloat16)
        part_up = jnp.dot(row_data.T, up_grad, preferred_element_type=jnp.float32).astype(jnp.bfloat16)
        part_down = jnp.dot(out_grad.T, hidden, preferred_element_type=jnp.float32).astype(jnp.bfloat16)
        sum_gate = sum_gate + part_gate.astype(jnp.float32)
        sum_up = sum_up + part_up.astype(jnp.float32)
        sum_down = sum_down + part_down.astype(jnp.float32)
        return (out_acc, grad_acc, gate_acc, sum_gate, sum_up, sum_down)

    def expert_step(running, expert):
        zeros_w = jnp.zeros((model_width, FF), jnp.float32)
        inside = (running[0], running[1], running[2], zeros_w, zeros_w, zeros_w)

        def column_step(state, column_index):
            return pair_step(state, column_index, expert), None

        inside, unused = lax.scan(column_step, inside, jnp.arange(COLUMNS, dtype=jnp.int32))
        return (inside[0], inside[1], inside[2]), (inside[3], inside[4], inside[5])

    initial = (jnp.zeros((TOKENS, model_width), jnp.float32),
               jnp.zeros((TOKENS, model_width), jnp.float32),
               jnp.zeros((slot_total,), jnp.float32))
    finished, weight_grads = lax.scan(expert_step, initial, jnp.arange(WINDOW, dtype=jnp.int32))
    output = finished[0].astype(jnp.bfloat16)
    grad_tokens = finished[1].astype(jnp.bfloat16)
    grad_gates = finished[2].reshape(TOKENS, TOP)
    return output, grad_tokens, grad_gates, weight_grads[0], weight_grads[1], weight_grads[2]
```

```python
import jax
import jax.numpy as jnp
from jax import lax
from jax.sharding import PartitionSpec as P

EXPERTS = 64
WAVE = 1
MOST = 48
F32 = jnp.float32
BF16 = jnp.bfloat16


def dot(a, b, dims):
    return lax.dot_general(a, b, (dims, ((), ())), preferred_element_type=F32)


def routes(expert_ids, gate_vals, groups):
    per_index = EXPERTS // groups
    window = WAVE * groups
    tok_count = expert_ids.shape[0]
    local_index = expert_ids % per_index
    window_slot = jnp.where(
        local_index < WAVE, expert_ids // per_index * WAVE + local_index, window
    )
    slot_is = window_slot[:, :, None] == jnp.arange(window, dtype=jnp.int32)[None, None, :]
    chosen = jnp.any(slot_is, axis=1)
    gate_of = jnp.sum(jnp.where(slot_is, gate_vals.astype(F32)[:, :, None], 0.0), axis=1)
    tok = jnp.arange(tok_count, dtype=jnp.int32)
    before = (tok[:, None] > tok[None, :]).astype(BF16)
    rank = dot(before, chosen.astype(BF16), ((1,), (0,))).astype(jnp.int32)
    place = chosen[:, :, None] & (
        rank[:, :, None] == jnp.arange(MOST, dtype=jnp.int32)[None, None, :]
    )
    pick = place.astype(BF16).reshape(tok_count, window * MOST)
    weighted = (
        jnp.where(place, gate_of[:, :, None], 0.0).astype(BF16).reshape(tok_count, window * MOST)
    )
    return slot_is, place, pick, weighted


def on_device(tokens, expert_ids, gate_vals, w_gate, w_up, w_down, cotangent):
    groups = lax.axis_size("expert")
    columns = lax.axis_size("fsdp")
    side = lax.axis_index("fsdp") % 2
    tok_count, width = tokens.shape
    block = w_gate.shape[1]
    rows = groups * MOST
    sides = [[i for i in range(columns) if i % 2 == s] for s in (0, 1)]
    pairs = [(i, i ^ 1) for i in range(columns)]

    def swap(x):
        return lax.ppermute(x, "fsdp", pairs)

    def gather(w):
        return lax.all_gather(w[0], "fsdp", axis_index_groups=sides, axis=0, tiled=True)

    def scatter(x):
        return lax.psum_scatter(
            x.astype(BF16), "fsdp", scatter_dimension=0, axis_index_groups=sides, tiled=True
        ).astype(F32)[None]

    def halves(x):
        cut = x.reshape(x.shape[0], columns // 2, 2, block)
        even = cut[:, :, 0].reshape(x.shape[0], width // 2)
        odd = cut[:, :, 1].reshape(x.shape[0], width // 2)
        return jnp.where(side == 0, even, odd), jnp.where(side == 0, odd, even)

    def whole_rows(mine, other):
        even = jnp.where(side == 0, mine, other).reshape(-1, columns // 2, 1, block)
        odd = jnp.where(side == 0, other, mine).reshape(-1, columns // 2, 1, block)
        return jnp.concatenate([even, odd], axis=2).reshape(-1, width)

    def exchange(mine, other):
        packed = jnp.stack(
            [mine.reshape(groups, MOST, width // 2), other.reshape(groups, MOST, width // 2)],
            axis=1,
        )
        there = lax.all_to_all(packed, "expert", split_axis=0, concat_axis=0, tiled=True)
        return there[:, 0].reshape(rows, width // 2), there[:, 1].reshape(rows, width // 2)

    full_gate, full_up, full_down = gather(w_gate), gather(w_up), gather(w_down)
    slot_is, place, pick, weighted = routes(expert_ids, gate_vals, groups)
    tok_mine, tok_other = halves(tokens)
    cot_mine, cot_other = halves(cotangent)
    first = ((0,), (0,))
    row_mine, row_other = exchange(
        dot(pick, tok_mine, first).astype(BF16), dot(pick, tok_other, first).astype(BF16)
    )
    og_mine, og_other = exchange(
        dot(weighted, cot_mine, first).astype(BF16), dot(weighted, cot_other, first).astype(BF16)
    )
    row_in = jnp.concatenate([row_mine, swap(row_other)], axis=0)
    out_grad = jnp.concatenate([og_mine, swap(og_other)], axis=0)

    def summed(x):
        return x[:rows] + swap(x[rows:].astype(BF16)).astype(F32)

    def both(x):
        return jnp.concatenate([x, swap(x)], axis=0)

    plain, turned = ((1,), (0,)), ((1,), (1,))
    gate_pre = summed(dot(row_in, full_gate, plain))
    up_pre = summed(dot(row_in, full_up, plain))
    sigmoid_g = jax.nn.sigmoid(gate_pre)
    hidden = both((gate_pre * sigmoid_g * up_pre).astype(BF16))
    grad_w_down = scatter(dot(out_grad, hidden, first))
    hidden_grad = summed(dot(out_grad, full_down, plain))
    gate_grad = both(
        (hidden_grad * up_pre * sigmoid_g * (1.0 + gate_pre * (1.0 - sigmoid_g))).astype(BF16)
    )
    grad_w_gate = scatter(dot(row_in, gate_grad, first))
    up_grad = both((hidden_grad * gate_pre * sigmoid_g).astype(BF16))
    grad_w_up = scatter(dot(row_in, up_grad, first))

    expert_out = dot(hidden, full_down, turned).astype(BF16)
    out_mine, out_other = exchange(expert_out[:rows], swap(expert_out[rows:]))
    slot_grad = (dot(gate_grad, full_gate, turned) + dot(up_grad, full_up, turned)).astype(BF16)
    sg_mine, sg_other = exchange(slot_grad[:rows], swap(slot_grad[rows:]))

    output = whole_rows(
        dot(weighted, out_mine, plain).astype(BF16), dot(weighted, out_other, plain).astype(BF16)
    )
    grad_tokens = whole_rows(
        dot(pick, sg_mine, plain).astype(BF16), dot(pick, sg_other, plain).astype(BF16)
    )
    met = dot(cot_mine, out_mine, turned) + dot(cot_other, out_other, turned)
    met = jnp.sum(jnp.where(place, met.reshape(place.shape), 0.0), axis=2)
    grad_gates = jnp.sum(jnp.where(slot_is, met[:, None, :], 0.0), axis=2)
    return (output, grad_tokens, grad_gates, grad_w_gate, grad_w_up, grad_w_down)


def solution(mesh):
    token = P(("expert", "fsdp"), None)
    weight = P("expert", "fsdp", None)
    return jax.shard_map(
        on_device,
        mesh=mesh,
        in_specs=(token, token, token, weight, weight, weight, token),
        out_specs=(token, token, token, weight, weight, weight),
        check_vma=False,
    )
```

```python
import functools

import jax
import jax.numpy as jnp
from jax import lax
from jax.experimental import pallas as pl
from jax.experimental.pallas import tpu as pltpu
from jax.sharding import PartitionSpec as P

EXPERTS = 64
WAVE = 1
MOST = 48
F32 = jnp.float32
BF16 = jnp.bfloat16


def dot(a, b, dims):
    return lax.dot_general(a, b, (dims, ((), ())), preferred_element_type=F32)


MESH = pl.DeviceIdType.MESH
HBM = pl.BlockSpec(memory_space=pltpu.MemorySpace.HBM)
VMEM = pl.BlockSpec(memory_space=pltpu.MemorySpace.VMEM)


class Place:
    def __init__(self, groups):
        self.groups = groups
        self.e = lax.axis_index("expert")
        f = lax.axis_index("fsdp")
        self.f = f
        self.chip = f // 2
        self.pair = f + 1 - 2 * (f % 2)
        bit_x, bit_y = self.chip % 2, self.chip // 2
        self.to_x, self.to_y = f + 2 - 4 * bit_x, f + 4 - 8 * bit_y
        self.chip_x, self.chip_y = self.chip + 1 - 2 * bit_x, self.chip + 2 - 4 * bit_y
        self.chip_far = 3 - self.chip

    def barrier(self, rows):
        sem = pltpu.get_barrier_semaphore()
        peers = [(self.e, self.to_x), (self.e, self.to_y)]
        if rows:
            for step in range(self.groups):
                there = (self.e + step) % self.groups
                peers.append((there, self.pair))
                if step:
                    peers.append((there, self.f))
        for peer in peers:
            pl.semaphore_signal(sem, inc=1, device_id=peer, device_id_type=MESH)
        pl.semaphore_wait(sem, len(peers))

    def rows(self, src, dst, which, send, recv, local):
        copies = []
        for half in range(2):
            for step in range(self.groups):
                there = (self.e + step) % self.groups
                if half == 0 and step == 0:
                    copy = pltpu.make_async_copy(
                        src.at[0, self.e], dst.at[0, self.e], local.at[which]
                    )
                else:
                    copy = pltpu.make_async_remote_copy(
                        src_ref=src.at[half, there],
                        dst_ref=dst.at[half, self.e],
                        send_sem=send.at[which, half, step],
                        recv_sem=recv.at[which, half, step],
                        device_id=(there, self.pair if half else self.f),
                        device_id_type=MESH,
                    )
                copy.start()
                copies.append(copy)
        return copies

    def send(self, src, dst, send, recv, index, to):
        copy = pltpu.make_async_remote_copy(
            src_ref=src,
            dst_ref=dst,
            send_sem=send.at[index],
            recv_sem=recv.at[index],
            device_id=(self.e, to),
            device_id_type=MESH,
        )
        copy.start()
        return copy


def gather_kernel(groups, count, n_rows, *refs):
    ws, xs = refs[:count], refs[count : count + n_rows]
    refs = refs[count + n_rows :]
    fulls, ins = refs[:count], refs[count : count + n_rows]
    ws_send, ws_recv, ws_local, x_send, x_recv, x_local = refs[count + n_rows :]
    at = Place(groups)
    half = ws[0].shape[0] // 2
    at.barrier(n_rows > 0)
    pending, first = [], []
    for j in range(n_rows):
        pending += at.rows(xs[j], ins[j], j, x_send, x_recv, x_local)
    for i in range(count):
        mine = fulls[i].at[at.chip]
        first.append(
            (
                at.send(ws[i], mine, ws_send, ws_recv, 4 * i, at.to_x),
                at.send(ws[i], mine, ws_send, ws_recv, 4 * i + 1, at.to_y),
            )
        )
        keep = pltpu.make_async_copy(ws[i], mine, ws_local.at[i])
        keep.start()
        pending.append(keep)
    for i in range(count):
        by_x, by_y = first[i]
        by_x.wait_recv()
        part = fulls[i].at[at.chip_x, pl.ds(0, half)]
        pending.append(at.send(part, part, ws_send, ws_recv, 4 * i + 2, at.to_y))
        by_y.wait_recv()
        part = fulls[i].at[at.chip_y, pl.ds(half, half)]
        pending.append(at.send(part, part, ws_send, ws_recv, 4 * i + 3, at.to_x))
        by_x.wait_send()
        by_y.wait_send()
    for copy in pending:
        copy.wait()


def gather_call(groups, ws, xs):
    count, n_rows = len(ws), len(xs)
    dma = pltpu.SemaphoreType.DMA
    return pl.pallas_call(
        functools.partial(gather_kernel, groups, count, n_rows),
        out_shape=[jax.ShapeDtypeStruct((4,) + w.shape, BF16) for w in ws]
        + [jax.ShapeDtypeStruct(x.shape, BF16) for x in xs],
        in_specs=[VMEM] * (count + n_rows),
        out_specs=[HBM] * (count + n_rows),
        scratch_shapes=[
            dma((4 * count,)),
            dma((4 * count,)),
            dma((count,)),
            dma((n_rows, 2, groups)),
            dma((n_rows, 2, groups)),
            dma((n_rows,)),
        ],
        compiler_params=pltpu.CompilerParams(
            collective_id=0, has_side_effects=True, vmem_limit_bytes=24 * 2**20
        ),
    )(*ws, *xs)


def scatter_kernel(groups, count, n_rows, *refs):
    ts, xs = refs[:count], refs[count : count + n_rows]
    refs = refs[count + n_rows :]
    from_x, from_y = refs[:count], refs[count : 2 * count]
    backs = refs[2 * count : 2 * count + n_rows]
    refs = refs[2 * count + n_rows :]
    far_x, far_y, sum_x, sum_y, t_send, t_recv, x_send, x_recv, x_local = refs
    at = Place(groups)
    half = far_x.shape[1]
    top, low = pl.ds(0, half), pl.ds(half, half)
    at.barrier(n_rows > 0)
    pending, first = [], []
    for i in range(count):
        first.append(
            (
                at.send(ts[i].at[at.chip_far, top], far_x.at[i], t_send, t_recv, 6 * i, at.to_x),
                at.send(
                    ts[i].at[at.chip_far, low], far_y.at[i], t_send, t_recv, 6 * i + 1, at.to_y
                ),
            )
        )
        pending.append(
            at.send(
                ts[i].at[at.chip_x, top], from_x[i].at[top], t_send, t_recv, 6 * i + 2, at.to_x
            )
        )
        pending.append(
            at.send(
                ts[i].at[at.chip_y, low], from_y[i].at[low], t_send, t_recv, 6 * i + 3, at.to_y
            )
        )
    for j in range(n_rows):
        pending += at.rows(xs[j], backs[j], j, x_send, x_recv, x_local)
    for i in range(count):
        by_x, by_y = first[i]
        by_x.wait_recv()
        sum_y[i] = (ts[i][at.chip_y, top].astype(F32) + far_x[i].astype(F32)).astype(BF16)
        pending.append(
            at.send(sum_y.at[i], from_y[i].at[top], t_send, t_recv, 6 * i + 4, at.to_y)
        )
        by_y.wait_recv()
        sum_x[i] = (ts[i][at.chip_x, low].astype(F32) + far_y[i].astype(F32)).astype(BF16)
        pending.append(
            at.send(sum_x.at[i], from_x[i].at[low], t_send, t_recv, 6 * i + 5, at.to_x)
        )
        by_x.wait_send()
        by_y.wait_send()
    for copy in pending:
        copy.wait()


def scatter_call(groups, ts, xs):
    count, n_rows = len(ts), len(xs)
    dma = pltpu.SemaphoreType.DMA
    block, ff = ts[0].shape[1:]
    piece = pltpu.VMEM((count, block // 2, ff), BF16)
    return pl.pallas_call(
        functools.partial(scatter_kernel, groups, count, n_rows),
        out_shape=[jax.ShapeDtypeStruct((block, ff), BF16)] * (2 * count)
        + [jax.ShapeDtypeStruct(x.shape, BF16) for x in xs],
        in_specs=[VMEM] * (count + n_rows),
        out_specs=[HBM] * (2 * count + n_rows),
        scratch_shapes=[piece] * 4
        + [
            dma((6 * count,)),
            dma((6 * count,)),
            dma((n_rows, 2, groups)),
            dma((n_rows, 2, groups)),
            dma((n_rows,)),
        ],
        compiler_params=pltpu.CompilerParams(
            collective_id=1, has_side_effects=True, vmem_limit_bytes=40 * 2**20
        ),
    )(*ts, *xs)


def routes(expert_ids, gate_vals, groups):
    per_index = EXPERTS // groups
    window = WAVE * groups
    tok_count = expert_ids.shape[0]
    local_index = expert_ids % per_index
    window_slot = jnp.where(
        local_index < WAVE, expert_ids // per_index * WAVE + local_index, window
    )
    slot_is = window_slot[:, :, None] == jnp.arange(window, dtype=jnp.int32)[None, None, :]
    chosen = jnp.any(slot_is, axis=1)
    gate_of = jnp.sum(jnp.where(slot_is, gate_vals.astype(F32)[:, :, None], 0.0), axis=1)
    tok = jnp.arange(tok_count, dtype=jnp.int32)
    before = (tok[:, None] > tok[None, :]).astype(BF16)
    rank = dot(before, chosen.astype(BF16), ((1,), (0,))).astype(jnp.int32)
    place = chosen[:, :, None] & (
        rank[:, :, None] == jnp.arange(MOST, dtype=jnp.int32)[None, None, :]
    )
    pick = place.astype(BF16).reshape(tok_count, window * MOST)
    weighted = (
        jnp.where(place, gate_of[:, :, None], 0.0).astype(BF16).reshape(tok_count, window * MOST)
    )
    return slot_is, place, pick, weighted


def on_device(tokens, expert_ids, gate_vals, w_gate, w_up, w_down, cotangent):
    groups = lax.axis_size("expert")
    columns = lax.axis_size("fsdp")
    side = lax.axis_index("fsdp") % 2
    tok_count, width = tokens.shape
    block = w_gate.shape[1]
    rows = groups * MOST
    sides = [[i for i in range(columns) if i % 2 == s] for s in (0, 1)]
    pairs = [(i, i ^ 1) for i in range(columns)]

    def swap(x):
        return lax.ppermute(x, "fsdp", pairs)

    def gather(w):
        return lax.all_gather(w[0], "fsdp", axis_index_groups=sides, axis=0, tiled=True)

    def scatter(x):
        return lax.psum_scatter(
            x.astype(BF16), "fsdp", scatter_dimension=0, axis_index_groups=sides, tiled=True
        ).astype(F32)[None]

    def halves(x):
        cut = x.reshape(x.shape[0], columns // 2, 2, block)
        even = cut[:, :, 0].reshape(x.shape[0], width // 2)
        odd = cut[:, :, 1].reshape(x.shape[0], width // 2)
        return jnp.where(side == 0, even, odd), jnp.where(side == 0, odd, even)

    def whole_rows(mine, other):
        even = jnp.where(side == 0, mine, other).reshape(-1, columns // 2, 1, block)
        odd = jnp.where(side == 0, other, mine).reshape(-1, columns // 2, 1, block)
        return jnp.concatenate([even, odd], axis=2).reshape(-1, width)

    def exchange(mine, other):
        packed = jnp.stack(
            [mine.reshape(groups, MOST, width // 2), other.reshape(groups, MOST, width // 2)],
            axis=1,
        )
        there = lax.all_to_all(packed, "expert", split_axis=0, concat_axis=0, tiled=True)
        return there[:, 0].reshape(rows, width // 2), there[:, 1].reshape(rows, width // 2)

    square = columns == 8
    slot_is, place, pick, weighted = routes(expert_ids, gate_vals, groups)
    tok_mine, tok_other = halves(tokens)
    cot_mine, cot_other = halves(cotangent)
    first = ((0,), (0,))
    send_rows = [
        dot(pick, tok_mine, first).astype(BF16),
        dot(pick, tok_other, first).astype(BF16),
        dot(weighted, cot_mine, first).astype(BF16),
        dot(weighted, cot_other, first).astype(BF16),
    ]
    if square:
        packed = [
            jnp.stack(send_rows[i : i + 2]).reshape(2, groups, MOST, width // 2) for i in (0, 2)
        ]
        *full, row_in, out_grad = gather_call(groups, [w_gate[0], w_up[0], w_down[0]], packed)
        full_gate, full_up, full_down = (w.reshape(width // 2, w.shape[2]) for w in full)
        row_in = row_in.reshape(2 * rows, width // 2)
        out_grad = out_grad.reshape(2 * rows, width // 2)
    else:
        full_gate, full_up, full_down = gather(w_gate), gather(w_up), gather(w_down)
        row_mine, row_other = exchange(*send_rows[:2])
        og_mine, og_other = exchange(*send_rows[2:])
        row_in = jnp.concatenate([row_mine, swap(row_other)], axis=0)
        out_grad = jnp.concatenate([og_mine, swap(og_other)], axis=0)

    def summed(x):
        return x[:rows] + swap(x[rows:].astype(BF16)).astype(F32)

    def both(x):
        return jnp.concatenate([x, swap(x)], axis=0)

    plain, turned = ((1,), (0,)), ((1,), (1,))
    gate_pre = summed(dot(row_in, full_gate, plain))
    up_pre = summed(dot(row_in, full_up, plain))
    sigmoid_g = jax.nn.sigmoid(gate_pre)
    hidden = both((gate_pre * sigmoid_g * up_pre).astype(BF16))
    grad_w_down = scatter(dot(out_grad, hidden, first))
    hidden_grad = summed(dot(out_grad, full_down, plain))
    gate_grad = both(
        (hidden_grad * up_pre * sigmoid_g * (1.0 + gate_pre * (1.0 - sigmoid_g))).astype(BF16)
    )
    up_grad = both((hidden_grad * gate_pre * sigmoid_g).astype(BF16))
    term_gate, term_up = dot(row_in, gate_grad, first), dot(row_in, up_grad, first)
    expert_out = dot(hidden, full_down, turned).astype(BF16)
    slot_grad = (dot(gate_grad, full_gate, turned) + dot(up_grad, full_up, turned)).astype(BF16)
    if square:
        terms = [t.astype(BF16).reshape(4, block, t.shape[1]) for t in (term_gate, term_up)]
        back = [r.reshape(2, groups, MOST, width // 2) for r in (expert_out, slot_grad)]
        gx, ux, gy, uy, out_back, sg_back = scatter_call(groups, terms, back)
        chip = lax.axis_index("fsdp") // 2

        def total(t, x, y):
            own = lax.dynamic_index_in_dim(t, chip, 0, keepdims=False).astype(F32)
            return (own + x.astype(F32) + y.astype(F32))[None]

        grad_w_gate, grad_w_up = total(terms[0], gx, gy), total(terms[1], ux, uy)
        out_mine, out_other = (out_back[i].reshape(rows, width // 2) for i in (0, 1))
        sg_mine, sg_other = (sg_back[i].reshape(rows, width // 2) for i in (0, 1))
    else:
        grad_w_gate, grad_w_up = scatter(term_gate), scatter(term_up)
        out_mine, out_other = exchange(expert_out[:rows], swap(expert_out[rows:]))
        sg_mine, sg_other = exchange(slot_grad[:rows], swap(slot_grad[rows:]))

    output = whole_rows(
        dot(weighted, out_mine, plain).astype(BF16), dot(weighted, out_other, plain).astype(BF16)
    )
    grad_tokens = whole_rows(
        dot(pick, sg_mine, plain).astype(BF16), dot(pick, sg_other, plain).astype(BF16)
    )
    met = dot(cot_mine, out_mine, turned) + dot(cot_other, out_other, turned)
    met = jnp.sum(jnp.where(place, met.reshape(place.shape), 0.0), axis=2)
    grad_gates = jnp.sum(jnp.where(slot_is, met[:, None, :], 0.0), axis=2)
    return (output, grad_tokens, grad_gates, grad_w_gate, grad_w_up, grad_w_down)


def solution(mesh):
    token = P(("expert", "fsdp"), None)
    weight = P("expert", "fsdp", None)
    return jax.shard_map(
        on_device,
        mesh=mesh,
        in_specs=(token, token, token, weight, weight, weight, token),
        out_specs=(token, token, token, weight, weight, weight),
        check_vma=False,
    )
```

```python
import functools

import jax
import jax.numpy as jnp
from jax import lax
from jax.experimental import pallas as pl
from jax.experimental.pallas import tpu as pltpu
from jax.sharding import PartitionSpec as P

EXPERTS = 64
WAVE = 1
MOST = 48
F32 = jnp.float32
BF16 = jnp.bfloat16


def dot(a, b, dims):
    return lax.dot_general(a, b, (dims, ((), ())), preferred_element_type=F32)


MESH = pl.DeviceIdType.MESH
HBM = pl.BlockSpec(memory_space=pltpu.MemorySpace.HBM)
VMEM = pl.BlockSpec(memory_space=pltpu.MemorySpace.VMEM)


class Place:
    def __init__(self, groups):
        self.groups = groups
        self.e = lax.axis_index("expert")
        f = lax.axis_index("fsdp")
        self.f = f
        self.chip = f // 2
        self.pair = f + 1 - 2 * (f % 2)
        bit_x, bit_y = self.chip % 2, self.chip // 2
        self.to_x, self.to_y = f + 2 - 4 * bit_x, f + 4 - 8 * bit_y
        self.chip_x, self.chip_y = self.chip + 1 - 2 * bit_x, self.chip + 2 - 4 * bit_y
        self.chip_far = 3 - self.chip

    def barrier(self, rows):
        sem = pltpu.get_barrier_semaphore()
        peers = [(self.e, self.to_x), (self.e, self.to_y)]
        if rows:
            for step in range(self.groups):
                there = (self.e + step) % self.groups
                peers.append((there, self.pair))
                if step:
                    peers.append((there, self.f))
        for peer in peers:
            pl.semaphore_signal(sem, inc=1, device_id=peer, device_id_type=MESH)
        pl.semaphore_wait(sem, len(peers))

    def rows(self, src, dst, which, send, recv, local):
        copies = []
        for half in range(2):
            for step in range(self.groups):
                there = (self.e + step) % self.groups
                if half == 0 and step == 0:
                    copy = pltpu.make_async_copy(
                        src.at[0, self.e], dst.at[0, self.e], local.at[which]
                    )
                else:
                    copy = pltpu.make_async_remote_copy(
                        src_ref=src.at[half, there],
                        dst_ref=dst.at[half, self.e],
                        send_sem=send.at[which, half, step],
                        recv_sem=recv.at[which, half, step],
                        device_id=(there, self.pair if half else self.f),
                        device_id_type=MESH,
                    )
                copy.start()
                copies.append(copy)
        return copies

    def send(self, src, dst, send, recv, index, to):
        copy = pltpu.make_async_remote_copy(
            src_ref=src,
            dst_ref=dst,
            send_sem=send.at[index],
            recv_sem=recv.at[index],
            device_id=(self.e, to),
            device_id_type=MESH,
        )
        copy.start()
        return copy


def gather_kernel(groups, count, n_rows, *refs):
    ws, picks = refs[:count], refs[count : count + n_rows]
    refs = refs[count + n_rows :]
    toks, refs = refs[:n_rows], refs[n_rows:]
    fulls, ins = refs[:count], refs[count : count + n_rows]
    xs, ws_send, ws_recv, ws_local, x_send, x_recv, x_local = refs[count + n_rows :]
    at = Place(groups)
    half = ws[0].shape[0] // 2
    at.barrier(n_rows > 0)
    pending, first = [], []
    for i in range(count):
        mine = fulls[i].at[at.chip]
        first.append(
            (
                at.send(ws[i], mine, ws_send, ws_recv, 4 * i, at.to_x),
                at.send(ws[i], mine, ws_send, ws_recv, 4 * i + 1, at.to_y),
            )
        )
        keep = pltpu.make_async_copy(ws[i], mine, ws_local.at[i])
        keep.start()
        pending.append(keep)
    block = ws[0].shape[0]
    for j in range(n_rows):
        for half_of in range(2):
            odd = at.f % 2 if half_of == 0 else 1 - at.f % 2
            for k in range(4):
                cols = pl.ds(pl.multiple_of((2 * k + odd) * block, block), block)
                part = dot(picks[j][...], toks[j][:, cols], ((0,), (0,))).astype(BF16)
                xs[j, half_of, :, :, pl.ds(k * block, block)] = part.reshape(
                    groups, MOST, block
                )
        pending += at.rows(xs.at[j], ins[j], j, x_send, x_recv, x_local)
    for i in range(count):
        by_x, by_y = first[i]
        by_x.wait_recv()
        part = fulls[i].at[at.chip_x, pl.ds(0, half)]
        pending.append(at.send(part, part, ws_send, ws_recv, 4 * i + 2, at.to_y))
        by_y.wait_recv()
        part = fulls[i].at[at.chip_y, pl.ds(half, half)]
        pending.append(at.send(part, part, ws_send, ws_recv, 4 * i + 3, at.to_x))
        by_x.wait_send()
        by_y.wait_send()
    for copy in pending:
        copy.wait()


def gather_call(groups, ws, picks, toks):
    count, n_rows = len(ws), len(toks)
    shape = (2, groups, MOST, toks[0].shape[1] // 2)
    dma = pltpu.SemaphoreType.DMA
    return pl.pallas_call(
        functools.partial(gather_kernel, groups, count, n_rows),
        out_shape=[jax.ShapeDtypeStruct((4,) + w.shape, BF16) for w in ws]
        + [jax.ShapeDtypeStruct(shape, BF16)] * n_rows,
        in_specs=[VMEM] * (count + 2 * n_rows),
        out_specs=[HBM] * (count + n_rows),
        scratch_shapes=[
            pltpu.VMEM((n_rows,) + shape, BF16),
            dma((4 * count,)),
            dma((4 * count,)),
            dma((count,)),
            dma((n_rows, 2, groups)),
            dma((n_rows, 2, groups)),
            dma((n_rows,)),
        ],
        compiler_params=pltpu.CompilerParams(
            collective_id=0, has_side_effects=True, vmem_limit_bytes=24 * 2**20
        ),
    )(*ws, *picks, *toks)


def scatter_kernel(groups, *refs):
    row_in, out_grad, hidden, gate_grad, up_grad, w_gate, w_up, w_down = refs[:8]
    owns, from_x, from_y, backs = refs[8:11], refs[11:14], refs[14:17], refs[17:19]
    term, xs, far_x, far_y, sum_x, sum_y, t_send, t_recv, x_send, x_recv, x_local = refs[19:]
    at = Place(groups)
    block = term.shape[2]
    half = block // 2
    top, low = pl.ds(0, half), pl.ds(half, half)
    at.barrier(True)
    pending, first = [], []
    factors = ((out_grad, hidden), (row_in, gate_grad), (row_in, up_grad))

    def product(i, chip):
        a, b = factors[i]
        cols = pl.ds(pl.multiple_of(chip * block, block), block)
        return dot(a[:, cols], b[...], ((0,), (0,))).astype(BF16)

    def send(i, n, src, dst, to):
        return at.send(src, dst, t_send, t_recv, 6 * i + n, to)

    for i in range(3):
        term[i, 0] = product(i, at.chip_far)
        first.append(
            (
                send(i, 0, term.at[i, 0, top], far_x.at[i], at.to_x),
                send(i, 1, term.at[i, 0, low], far_y.at[i], at.to_y),
            )
        )
        term[i, 1] = product(i, at.chip_x)
        pending.append(send(i, 2, term.at[i, 1, top], from_x[i].at[top], at.to_x))
        term[i, 2] = product(i, at.chip_y)
        pending.append(send(i, 3, term.at[i, 2, low], from_y[i].at[low], at.to_y))
    turned = ((1,), (1,))
    back = dot(hidden[...], w_down[...], turned).astype(BF16)
    xs[0] = back.reshape(xs.shape[1:])
    pending += at.rows(xs.at[0], backs[0], 0, x_send, x_recv, x_local)
    back = dot(gate_grad[...], w_gate[...], turned) + dot(up_grad[...], w_up[...], turned)
    xs[1] = back.astype(BF16).reshape(xs.shape[1:])
    pending += at.rows(xs.at[1], backs[1], 1, x_send, x_recv, x_local)
    for i in range(3):
        by_x, by_y = first[i]
        by_x.wait_recv()
        sum_y[i] = (term[i, 2, top].astype(F32) + far_x[i].astype(F32)).astype(BF16)
        pending.append(send(i, 4, sum_y.at[i], from_y[i].at[top], at.to_y))
        by_y.wait_recv()
        sum_x[i] = (term[i, 1, low].astype(F32) + far_y[i].astype(F32)).astype(BF16)
        pending.append(send(i, 5, sum_x.at[i], from_x[i].at[low], at.to_x))
        owns[i][...] = product(i, at.chip)
        by_x.wait_send()
        by_y.wait_send()
    for copy in pending:
        copy.wait()


def scatter_call(groups, block, row_in, out_grad, acts, ws):
    dma = pltpu.SemaphoreType.DMA
    ff = acts[0].shape[1]
    shape = (2, groups, MOST, row_in.shape[1])
    piece = pltpu.VMEM((3, block // 2, ff), BF16)
    return pl.pallas_call(
        functools.partial(scatter_kernel, groups),
        out_shape=[jax.ShapeDtypeStruct((block, ff), BF16)] * 9
        + [jax.ShapeDtypeStruct(shape, BF16)] * 2,
        in_specs=[VMEM] * 8,
        out_specs=[VMEM] * 3 + [HBM] * 8,
        scratch_shapes=[
            pltpu.VMEM((3, 3, block, ff), BF16),
            pltpu.VMEM((2,) + shape, BF16),
            piece,
            piece,
            piece,
            piece,
            dma((18,)),
            dma((18,)),
            dma((2, 2, groups)),
            dma((2, 2, groups)),
            dma((2,)),
        ],
        compiler_params=pltpu.CompilerParams(
            collective_id=1, has_side_effects=True, vmem_limit_bytes=48 * 2**20
        ),
    )(row_in, out_grad, *acts, *ws)


def routes(expert_ids, gate_vals, groups):
    per_index = EXPERTS // groups
    window = WAVE * groups
    tok_count = expert_ids.shape[0]
    local_index = expert_ids % per_index
    window_slot = jnp.where(
        local_index < WAVE, expert_ids // per_index * WAVE + local_index, window
    )
    slot_is = window_slot[:, :, None] == jnp.arange(window, dtype=jnp.int32)[None, None, :]
    chosen = jnp.any(slot_is, axis=1)
    gate_of = jnp.sum(jnp.where(slot_is, gate_vals.astype(F32)[:, :, None], 0.0), axis=1)
    tok = jnp.arange(tok_count, dtype=jnp.int32)
    before = (tok[:, None] > tok[None, :]).astype(BF16)
    rank = dot(before, chosen.astype(BF16), ((1,), (0,))).astype(jnp.int32)
    place = chosen[:, :, None] & (
        rank[:, :, None] == jnp.arange(MOST, dtype=jnp.int32)[None, None, :]
    )
    pick = place.astype(BF16).reshape(tok_count, window * MOST)
    weighted = (
        jnp.where(place, gate_of[:, :, None], 0.0).astype(BF16).reshape(tok_count, window * MOST)
    )
    return slot_is, place, pick, weighted


def on_device(tokens, expert_ids, gate_vals, w_gate, w_up, w_down, cotangent):
    groups = lax.axis_size("expert")
    columns = lax.axis_size("fsdp")
    side = lax.axis_index("fsdp") % 2
    tok_count, width = tokens.shape
    block = w_gate.shape[1]
    rows = groups * MOST
    sides = [[i for i in range(columns) if i % 2 == s] for s in (0, 1)]
    pairs = [(i, i ^ 1) for i in range(columns)]

    def swap(x):
        return lax.ppermute(x, "fsdp", pairs)

    def gather(w):
        return lax.all_gather(w[0], "fsdp", axis_index_groups=sides, axis=0, tiled=True)

    def scatter(x):
        return lax.psum_scatter(
            x.astype(BF16), "fsdp", scatter_dimension=0, axis_index_groups=sides, tiled=True
        ).astype(F32)[None]

    def cut(x, odd):
        return jnp.concatenate(
            [x[:, (2 * k + odd) * block : (2 * k + odd + 1) * block] for k in range(columns // 2)],
            axis=1,
        )

    def halves(x):
        even, odd = cut(x, 0), cut(x, 1)
        return jnp.where(side == 0, even, odd), jnp.where(side == 0, odd, even)

    def whole_rows(mine, other):
        even, odd = jnp.where(side == 0, mine, other), jnp.where(side == 0, other, mine)
        parts = []
        for k in range(columns // 2):
            here = slice(k * block, (k + 1) * block)
            parts += [even[:, here], odd[:, here]]
        return jnp.concatenate(parts, axis=1)

    def exchange(mine, other):
        packed = jnp.stack(
            [mine.reshape(groups, MOST, width // 2), other.reshape(groups, MOST, width // 2)],
            axis=1,
        )
        there = lax.all_to_all(packed, "expert", split_axis=0, concat_axis=0, tiled=True)
        return there[:, 0].reshape(rows, width // 2), there[:, 1].reshape(rows, width // 2)

    square = columns == 8
    slot_is, place, pick, weighted = routes(expert_ids, gate_vals, groups)
    first = ((0,), (0,))
    if square:
        *full, row_in, out_grad = gather_call(
            groups, [w_gate[0], w_up[0], w_down[0]], [pick, weighted], [tokens, cotangent]
        )
        full_gate, full_up, full_down = (w.reshape(width // 2, w.shape[2]) for w in full)
        row_in = row_in.reshape(2 * rows, width // 2)
        out_grad = out_grad.reshape(2 * rows, width // 2)
    else:
        full_gate, full_up, full_down = gather(w_gate), gather(w_up), gather(w_down)
        row_mine, row_other = exchange(*halves(dot(pick, tokens, first).astype(BF16)))
        og_mine, og_other = exchange(*halves(dot(weighted, cotangent, first).astype(BF16)))
        row_in = jnp.concatenate([row_mine, swap(row_other)], axis=0)
        out_grad = jnp.concatenate([og_mine, swap(og_other)], axis=0)

    def summed(x):
        return x[:rows] + swap(x[rows:].astype(BF16)).astype(F32)

    def both(x):
        return jnp.concatenate([x, swap(x)], axis=0)

    plain, turned = ((1,), (0,)), ((1,), (1,))
    gate_pre = summed(dot(row_in, full_gate, plain))
    up_pre = summed(dot(row_in, full_up, plain))
    sigmoid_g = jax.nn.sigmoid(gate_pre)
    hidden = both((gate_pre * sigmoid_g * up_pre).astype(BF16))
    hidden_grad = summed(dot(out_grad, full_down, plain))
    gate_grad = both(
        (hidden_grad * up_pre * sigmoid_g * (1.0 + gate_pre * (1.0 - sigmoid_g))).astype(BF16)
    )
    up_grad = both((hidden_grad * gate_pre * sigmoid_g).astype(BF16))
    if square:
        got = scatter_call(
            groups,
            block,
            row_in,
            out_grad,
            [hidden, gate_grad, up_grad],
            [full_gate, full_up, full_down],
        )
        grad_w_down, grad_w_gate, grad_w_up = (
            (got[i].astype(F32) + got[3 + i].astype(F32) + got[6 + i].astype(F32))[None]
            for i in range(3)
        )
        outs, grads = ([r[i].reshape(rows, width // 2) for i in (0, 1)] for r in got[9:])
    else:
        grad_w_down = scatter(dot(out_grad, hidden, first))
        grad_w_gate = scatter(dot(row_in, gate_grad, first))
        grad_w_up = scatter(dot(row_in, up_grad, first))
        expert_out = dot(hidden, full_down, turned).astype(BF16)
        slot_grad = (
            dot(gate_grad, full_gate, turned) + dot(up_grad, full_up, turned)
        ).astype(BF16)
        outs = exchange(expert_out[:rows], swap(expert_out[rows:]))
        grads = exchange(slot_grad[:rows], swap(slot_grad[rows:]))

    slot_out = whole_rows(*outs)
    output = dot(weighted, slot_out, plain).astype(BF16)
    grad_tokens = dot(pick, whole_rows(*grads), plain).astype(BF16)
    met = dot(cotangent, slot_out, turned)
    met = jnp.sum(jnp.where(place, met.reshape(place.shape), 0.0), axis=2)
    grad_gates = jnp.sum(jnp.where(slot_is, met[:, None, :], 0.0), axis=2)
    return (output, grad_tokens, grad_gates, grad_w_gate, grad_w_up, grad_w_down)


def solution(mesh):
    token = P(("expert", "fsdp"), None)
    weight = P("expert", "fsdp", None)
    return jax.shard_map(
        on_device,
        mesh=mesh,
        in_specs=(token, token, token, weight, weight, weight, token),
        out_specs=(token, token, token, weight, weight, weight),
        check_vma=False,
    )
```

```python
import functools

import jax
import jax.numpy as jnp
from jax import lax
from jax.experimental import pallas as pl
from jax.experimental.pallas import tpu as pltpu
from jax.sharding import PartitionSpec as P

EXPERTS = 64
WAVE = 1
MOST = 48
F32 = jnp.float32
BF16 = jnp.bfloat16


def dot(a, b, dims):
    return lax.dot_general(a, b, (dims, ((), ())), preferred_element_type=F32)


MESH = pl.DeviceIdType.MESH
HBM = pl.BlockSpec(memory_space=pltpu.MemorySpace.HBM)
VMEM = pl.BlockSpec(memory_space=pltpu.MemorySpace.VMEM)


class Place:
    def __init__(self, groups):
        self.groups = groups
        self.e = lax.axis_index("expert")
        f = lax.axis_index("fsdp")
        self.f = f
        self.chip = f // 2
        self.pair = f + 1 - 2 * (f % 2)
        bit_x, bit_y = self.chip % 2, self.chip // 2
        self.to_x, self.to_y = f + 2 - 4 * bit_x, f + 4 - 8 * bit_y
        self.chip_x, self.chip_y = self.chip + 1 - 2 * bit_x, self.chip + 2 - 4 * bit_y
        self.chip_far = 3 - self.chip

    def barrier(self, rows):
        sem = pltpu.get_barrier_semaphore()
        peers = [(self.e, self.to_x), (self.e, self.to_y)]
        if rows:
            for step in range(self.groups):
                there = (self.e + step) % self.groups
                peers.append((there, self.pair))
                if step:
                    peers.append((there, self.f))
        for peer in peers:
            pl.semaphore_signal(sem, inc=1, device_id=peer, device_id_type=MESH)
        pl.semaphore_wait(sem, len(peers))

    def rows(self, src, dst, which, send, recv, local):
        copies = []
        for half in range(2):
            for step in range(self.groups):
                there = (self.e + step) % self.groups
                if half == 0 and step == 0:
                    copy = pltpu.make_async_copy(
                        src.at[0, self.e], dst.at[0, self.e], local.at[which]
                    )
                else:
                    copy = pltpu.make_async_remote_copy(
                        src_ref=src.at[half, there],
                        dst_ref=dst.at[half, self.e],
                        send_sem=send.at[which, half, step],
                        recv_sem=recv.at[which, half, step],
                        device_id=(there, self.pair if half else self.f),
                        device_id_type=MESH,
                    )
                copy.start()
                copies.append(copy)
        return copies

    def send(self, src, dst, send, recv, index, to):
        copy = pltpu.make_async_remote_copy(
            src_ref=src,
            dst_ref=dst,
            send_sem=send.at[index],
            recv_sem=recv.at[index],
            device_id=(self.e, to),
            device_id_type=MESH,
        )
        copy.start()
        return copy


def gather_kernel(groups, count, n_rows, *refs):
    ws, picks = refs[:count], refs[count : count + n_rows]
    refs = refs[count + n_rows :]
    toks, refs = refs[:n_rows], refs[n_rows:]
    fulls, ins = refs[:count], refs[count : count + n_rows]
    xs, ws_send, ws_recv, ws_local, x_send, x_recv, x_local = refs[count + n_rows :]
    at = Place(groups)
    half = ws[0].shape[0] // 2
    at.barrier(n_rows > 0)
    pending, first = [], []
    for i in range(count):
        mine = fulls[i].at[at.chip]
        first.append(
            (
                at.send(ws[i], mine, ws_send, ws_recv, 4 * i, at.to_x),
                at.send(ws[i], mine, ws_send, ws_recv, 4 * i + 1, at.to_y),
            )
        )
        keep = pltpu.make_async_copy(ws[i], mine, ws_local.at[i])
        keep.start()
        pending.append(keep)
    block = ws[0].shape[0]
    for j in range(n_rows):
        for half_of in range(2):
            odd = at.f % 2 if half_of == 0 else 1 - at.f % 2
            for k in range(4):
                cols = pl.ds(pl.multiple_of((2 * k + odd) * block, block), block)
                part = dot(picks[j][...], toks[j][:, cols], ((0,), (0,))).astype(BF16)
                xs[j, half_of, :, :, pl.ds(k * block, block)] = part.reshape(
                    groups, MOST, block
                )
        pending += at.rows(xs.at[j], ins[j], j, x_send, x_recv, x_local)
    for i in range(count):
        by_x, by_y = first[i]
        by_x.wait_recv()
        part = fulls[i].at[at.chip_x, pl.ds(0, half)]
        pending.append(at.send(part, part, ws_send, ws_recv, 4 * i + 2, at.to_y))
        by_y.wait_recv()
        part = fulls[i].at[at.chip_y, pl.ds(half, half)]
        pending.append(at.send(part, part, ws_send, ws_recv, 4 * i + 3, at.to_x))
        by_x.wait_send()
        by_y.wait_send()
    for copy in pending:
        copy.wait()


def gather_call(groups, ws, picks, toks):
    count, n_rows = len(ws), len(toks)
    shape = (2, groups, MOST, toks[0].shape[1] // 2)
    dma = pltpu.SemaphoreType.DMA
    return pl.pallas_call(
        functools.partial(gather_kernel, groups, count, n_rows),
        out_shape=[jax.ShapeDtypeStruct((4,) + w.shape, BF16) for w in ws]
        + [jax.ShapeDtypeStruct(shape, BF16)] * n_rows,
        in_specs=[VMEM] * (count + 2 * n_rows),
        out_specs=[HBM] * (count + n_rows),
        scratch_shapes=[
            pltpu.VMEM((n_rows,) + shape, BF16),
            dma((4 * count,)),
            dma((4 * count,)),
            dma((count,)),
            dma((n_rows, 2, groups)),
            dma((n_rows, 2, groups)),
            dma((n_rows,)),
        ],
        compiler_params=pltpu.CompilerParams(
            collective_id=0, has_side_effects=True, vmem_limit_bytes=24 * 2**20
        ),
    )(*ws, *picks, *toks)


def scatter_kernel(groups, *refs):
    row_in, out_grad, hidden, gate_grad, up_grad, w_gate, w_up, w_down = refs[:8]
    owns, from_x, from_y, backs = refs[8:11], refs[11:14], refs[14:17], refs[17:19]
    term, xs, far_x, far_y, sum_x, sum_y, others = refs[19:26]
    t_send, t_recv, x_send, x_recv, x_local, a_send, a_recv = refs[26:]
    at = Place(groups)
    block = term.shape[2]
    half = block // 2
    top, low = pl.ds(0, half), pl.ds(half, half)
    at.barrier(True)
    pending, first = [], []
    factors = ((out_grad, hidden), (row_in, gate_grad), (row_in, up_grad))
    rows = hidden.shape[0]
    swaps = [
        at.send(act, others.at[i], a_send, a_recv, i, at.pair)
        for i, (_, act) in enumerate(factors)
    ]

    def product(i, chip):
        a, b = factors[i]
        cols = pl.ds(pl.multiple_of(chip * block, block), block)
        own = dot(a[pl.ds(0, rows), cols], b[...], ((0,), (0,)))
        return (own + dot(a[pl.ds(rows, rows), cols], others[i], ((0,), (0,)))).astype(BF16)

    def send(i, n, src, dst, to):
        return at.send(src, dst, t_send, t_recv, 6 * i + n, to)

    for i in range(3):
        swaps[i].wait()
        term[i, 0] = product(i, at.chip_far)
        first.append(
            (
                send(i, 0, term.at[i, 0, top], far_x.at[i], at.to_x),
                send(i, 1, term.at[i, 0, low], far_y.at[i], at.to_y),
            )
        )
        term[i, 1] = product(i, at.chip_x)
        pending.append(send(i, 2, term.at[i, 1, top], from_x[i].at[top], at.to_x))
        term[i, 2] = product(i, at.chip_y)
        pending.append(send(i, 3, term.at[i, 2, low], from_y[i].at[low], at.to_y))
    turned = ((1,), (1,))
    for slot in range(2):
        act = others[0] if slot else hidden[...]
        xs[0, slot] = dot(act, w_down[...], turned).astype(BF16).reshape(xs.shape[2:])
    pending += at.rows(xs.at[0], backs[0], 0, x_send, x_recv, x_local)
    for slot in range(2):
        g, u = (others[1], others[2]) if slot else (gate_grad[...], up_grad[...])
        back = dot(g, w_gate[...], turned) + dot(u, w_up[...], turned)
        xs[1, slot] = back.astype(BF16).reshape(xs.shape[2:])
    pending += at.rows(xs.at[1], backs[1], 1, x_send, x_recv, x_local)
    for i in range(3):
        by_x, by_y = first[i]
        by_x.wait_recv()
        sum_y[i] = (term[i, 2, top].astype(F32) + far_x[i].astype(F32)).astype(BF16)
        pending.append(send(i, 4, sum_y.at[i], from_y[i].at[top], at.to_y))
        by_y.wait_recv()
        sum_x[i] = (term[i, 1, low].astype(F32) + far_y[i].astype(F32)).astype(BF16)
        pending.append(send(i, 5, sum_x.at[i], from_x[i].at[low], at.to_x))
        owns[i][...] = product(i, at.chip)
        by_x.wait_send()
        by_y.wait_send()
    for copy in pending:
        copy.wait()


def scatter_call(groups, block, row_in, out_grad, acts, ws):
    dma = pltpu.SemaphoreType.DMA
    ff = acts[0].shape[1]
    shape = (2, groups, MOST, row_in.shape[1])
    piece = pltpu.VMEM((3, block // 2, ff), BF16)
    return pl.pallas_call(
        functools.partial(scatter_kernel, groups),
        out_shape=[jax.ShapeDtypeStruct((block, ff), BF16)] * 9
        + [jax.ShapeDtypeStruct(shape, BF16)] * 2,
        in_specs=[VMEM] * 8,
        out_specs=[VMEM] * 3 + [HBM] * 8,
        scratch_shapes=[
            pltpu.VMEM((3, 3, block, ff), BF16),
            pltpu.VMEM((2,) + shape, BF16),
            piece,
            piece,
            piece,
            piece,
            pltpu.VMEM((3,) + acts[0].shape, BF16),
            dma((18,)),
            dma((18,)),
            dma((2, 2, groups)),
            dma((2, 2, groups)),
            dma((2,)),
            dma((3,)),
            dma((3,)),
        ],
        compiler_params=pltpu.CompilerParams(
            collective_id=1, has_side_effects=True, vmem_limit_bytes=48 * 2**20
        ),
    )(row_in, out_grad, *acts, *ws)


def routes(expert_ids, gate_vals, groups):
    per_index = EXPERTS // groups
    window = WAVE * groups
    tok_count = expert_ids.shape[0]
    local_index = expert_ids % per_index
    window_slot = jnp.where(
        local_index < WAVE, expert_ids // per_index * WAVE + local_index, window
    )
    slot_is = window_slot[:, :, None] == jnp.arange(window, dtype=jnp.int32)[None, None, :]
    chosen = jnp.any(slot_is, axis=1)
    gate_of = jnp.sum(jnp.where(slot_is, gate_vals.astype(F32)[:, :, None], 0.0), axis=1)
    tok = jnp.arange(tok_count, dtype=jnp.int32)
    before = (tok[:, None] > tok[None, :]).astype(BF16)
    rank = dot(before, chosen.astype(BF16), ((1,), (0,))).astype(jnp.int32)
    place = chosen[:, :, None] & (
        rank[:, :, None] == jnp.arange(MOST, dtype=jnp.int32)[None, None, :]
    )
    pick = place.astype(BF16).reshape(tok_count, window * MOST)
    weighted = (
        jnp.where(place, gate_of[:, :, None], 0.0).astype(BF16).reshape(tok_count, window * MOST)
    )
    return slot_is, place, pick, weighted


def on_device(tokens, expert_ids, gate_vals, w_gate, w_up, w_down, cotangent):
    groups = lax.axis_size("expert")
    columns = lax.axis_size("fsdp")
    side = lax.axis_index("fsdp") % 2
    tok_count, width = tokens.shape
    block = w_gate.shape[1]
    rows = groups * MOST
    sides = [[i for i in range(columns) if i % 2 == s] for s in (0, 1)]
    pairs = [(i, i ^ 1) for i in range(columns)]

    def swap(x):
        return lax.ppermute(x, "fsdp", pairs)

    def gather(w):
        return lax.all_gather(w[0], "fsdp", axis_index_groups=sides, axis=0, tiled=True)

    def scatter(x):
        return lax.psum_scatter(
            x.astype(BF16), "fsdp", scatter_dimension=0, axis_index_groups=sides, tiled=True
        ).astype(F32)[None]

    def cut(x, odd):
        return jnp.concatenate(
            [x[:, (2 * k + odd) * block : (2 * k + odd + 1) * block] for k in range(columns // 2)],
            axis=1,
        )

    def halves(x):
        even, odd = cut(x, 0), cut(x, 1)
        return jnp.where(side == 0, even, odd), jnp.where(side == 0, odd, even)

    def whole_rows(mine, other):
        even, odd = jnp.where(side == 0, mine, other), jnp.where(side == 0, other, mine)
        parts = []
        for k in range(columns // 2):
            here = slice(k * block, (k + 1) * block)
            parts += [even[:, here], odd[:, here]]
        return jnp.concatenate(parts, axis=1)

    def exchange(mine, other):
        packed = jnp.stack(
            [mine.reshape(groups, MOST, width // 2), other.reshape(groups, MOST, width // 2)],
            axis=1,
        )
        there = lax.all_to_all(packed, "expert", split_axis=0, concat_axis=0, tiled=True)
        return there[:, 0].reshape(rows, width // 2), there[:, 1].reshape(rows, width // 2)

    square = columns == 8
    slot_is, place, pick, weighted = routes(expert_ids, gate_vals, groups)
    first = ((0,), (0,))
    if square:
        *full, row_in, out_grad = gather_call(
            groups, [w_gate[0], w_up[0], w_down[0]], [pick, weighted], [tokens, cotangent]
        )
        full_gate, full_up, full_down = (w.reshape(width // 2, w.shape[2]) for w in full)
        row_in = row_in.reshape(2 * rows, width // 2)
        out_grad = out_grad.reshape(2 * rows, width // 2)
    else:
        full_gate, full_up, full_down = gather(w_gate), gather(w_up), gather(w_down)
        row_mine, row_other = exchange(*halves(dot(pick, tokens, first).astype(BF16)))
        og_mine, og_other = exchange(*halves(dot(weighted, cotangent, first).astype(BF16)))
        row_in = jnp.concatenate([row_mine, swap(row_other)], axis=0)
        out_grad = jnp.concatenate([og_mine, swap(og_other)], axis=0)

    def summed(x):
        return x[:rows] + swap(x[rows:].astype(BF16)).astype(F32)

    def both(x):
        return jnp.concatenate([x, swap(x)], axis=0)

    plain, turned = ((1,), (0,)), ((1,), (1,))
    gate_pre = summed(dot(row_in, full_gate, plain))
    up_pre = summed(dot(row_in, full_up, plain))
    sigmoid_g = jax.nn.sigmoid(gate_pre)
    hidden = (gate_pre * sigmoid_g * up_pre).astype(BF16)
    hidden_grad = summed(dot(out_grad, full_down, plain))
    gate_grad = (
        hidden_grad * up_pre * sigmoid_g * (1.0 + gate_pre * (1.0 - sigmoid_g))
    ).astype(BF16)
    up_grad = (hidden_grad * gate_pre * sigmoid_g).astype(BF16)
    if square:
        got = scatter_call(
            groups,
            block,
            row_in,
            out_grad,
            [hidden, gate_grad, up_grad],
            [full_gate, full_up, full_down],
        )
        grad_w_down, grad_w_gate, grad_w_up = (
            (got[i].astype(F32) + got[3 + i].astype(F32) + got[6 + i].astype(F32))[None]
            for i in range(3)
        )
        outs, grads = ([r[i].reshape(rows, width // 2) for i in (0, 1)] for r in got[9:])
    else:
        hidden, gate_grad, up_grad = both(hidden), both(gate_grad), both(up_grad)
        grad_w_down = scatter(dot(out_grad, hidden, first))
        grad_w_gate = scatter(dot(row_in, gate_grad, first))
        grad_w_up = scatter(dot(row_in, up_grad, first))
        expert_out = dot(hidden, full_down, turned).astype(BF16)
        slot_grad = (
            dot(gate_grad, full_gate, turned) + dot(up_grad, full_up, turned)
        ).astype(BF16)
        outs = exchange(expert_out[:rows], swap(expert_out[rows:]))
        grads = exchange(slot_grad[:rows], swap(slot_grad[rows:]))

    slot_out = whole_rows(*outs)
    output = dot(weighted, slot_out, plain).astype(BF16)
    grad_tokens = dot(pick, whole_rows(*grads), plain).astype(BF16)
    met = dot(cotangent, slot_out, turned)
    met = jnp.sum(jnp.where(place, met.reshape(place.shape), 0.0), axis=2)
    grad_gates = jnp.sum(jnp.where(slot_is, met[:, None, :], 0.0), axis=2)
    return (output, grad_tokens, grad_gates, grad_w_gate, grad_w_up, grad_w_down)


def solution(mesh):
    token = P(("expert", "fsdp"), None)
    weight = P("expert", "fsdp", None)
    return jax.shard_map(
        on_device,
        mesh=mesh,
        in_specs=(token, token, token, weight, weight, weight, token),
        out_specs=(token, token, token, weight, weight, weight),
        check_vma=False,
    )
```

```python
import functools

import jax
import jax.numpy as jnp
from jax import lax
from jax.experimental import pallas as pl
from jax.experimental.pallas import tpu as pltpu
from jax.sharding import PartitionSpec as P

EXPERTS = 64
WAVE = 1
MOST = 48
F32 = jnp.float32
BF16 = jnp.bfloat16


def dot(a, b, dims):
    return lax.dot_general(a, b, (dims, ((), ())), preferred_element_type=F32)


MESH = pl.DeviceIdType.MESH
HBM = pl.BlockSpec(memory_space=pltpu.MemorySpace.HBM)
VMEM = pl.BlockSpec(memory_space=pltpu.MemorySpace.VMEM)


class Place:
    def __init__(self, groups):
        self.groups = groups
        self.e = lax.axis_index("expert")
        f = lax.axis_index("fsdp")
        self.f = f
        self.chip = f // 2
        self.pair = f + 1 - 2 * (f % 2)
        bit_x, bit_y = self.chip % 2, self.chip // 2
        self.to_x, self.to_y = f + 2 - 4 * bit_x, f + 4 - 8 * bit_y
        self.chip_x, self.chip_y = self.chip + 1 - 2 * bit_x, self.chip + 2 - 4 * bit_y
        self.chip_far = 3 - self.chip

    def barrier(self, rows):
        sem = pltpu.get_barrier_semaphore()
        peers = [(self.e, self.to_x), (self.e, self.to_y)]
        if rows:
            for step in range(self.groups):
                there = (self.e + step) % self.groups
                peers.append((there, self.pair))
                if step:
                    peers.append((there, self.f))
        for peer in peers:
            pl.semaphore_signal(sem, inc=1, device_id=peer, device_id_type=MESH)
        pl.semaphore_wait(sem, len(peers))

    def rows(self, src, dst, which, send, recv, local):
        copies = []
        for half in range(2):
            for step in range(self.groups):
                there = (self.e + step) % self.groups
                if half == 0 and step == 0:
                    copy = pltpu.make_async_copy(
                        src.at[0, self.e], dst.at[0, self.e], local.at[which]
                    )
                else:
                    copy = pltpu.make_async_remote_copy(
                        src_ref=src.at[half, there],
                        dst_ref=dst.at[half, self.e],
                        send_sem=send.at[which, half, step],
                        recv_sem=recv.at[which, half, step],
                        device_id=(there, self.pair if half else self.f),
                        device_id_type=MESH,
                    )
                copy.start()
                copies.append(copy)
        return copies

    def send(self, src, dst, send, recv, index, to):
        copy = pltpu.make_async_remote_copy(
            src_ref=src,
            dst_ref=dst,
            send_sem=send.at[index],
            recv_sem=recv.at[index],
            device_id=(self.e, to),
            device_id_type=MESH,
        )
        copy.start()
        return copy


def gather_kernel(groups, count, n_rows, *refs):
    ws, picks = refs[:count], refs[count : count + n_rows]
    refs = refs[count + n_rows :]
    toks, refs = refs[:n_rows], refs[n_rows:]
    fulls, ins = refs[:count], refs[count : count + n_rows]
    xs, ws_send, ws_recv, ws_local, x_send, x_recv, x_local = refs[count + n_rows :]
    at = Place(groups)
    half = ws[0].shape[0] // 2
    at.barrier(n_rows > 0)
    pending, first = [], []
    for i in range(count):
        mine = fulls[i].at[at.chip]
        first.append(
            (
                at.send(ws[i], mine, ws_send, ws_recv, 4 * i, at.to_x),
                at.send(ws[i], mine, ws_send, ws_recv, 4 * i + 1, at.to_y),
            )
        )
        keep = pltpu.make_async_copy(ws[i], mine, ws_local.at[i])
        keep.start()
        pending.append(keep)
    block = ws[0].shape[0]
    for j in range(n_rows):
        for half_of in range(2):
            odd = at.f % 2 if half_of == 0 else 1 - at.f % 2
            for k in range(4):
                cols = pl.ds(pl.multiple_of((2 * k + odd) * block, block), block)
                part = dot(picks[j][...], toks[j][:, cols], ((0,), (0,))).astype(BF16)
                xs[j, half_of, :, :, pl.ds(k * block, block)] = part.reshape(
                    groups, MOST, block
                )
        pending += at.rows(xs.at[j], ins[j], j, x_send, x_recv, x_local)
    for i in range(count):
        by_x, by_y = first[i]
        by_x.wait_recv()
        part = fulls[i].at[at.chip_x, pl.ds(0, half)]
        pending.append(at.send(part, part, ws_send, ws_recv, 4 * i + 2, at.to_y))
        by_y.wait_recv()
        part = fulls[i].at[at.chip_y, pl.ds(half, half)]
        pending.append(at.send(part, part, ws_send, ws_recv, 4 * i + 3, at.to_x))
        by_x.wait_send()
        by_y.wait_send()
    for copy in pending:
        copy.wait()


def gather_call(groups, ws, picks, toks):
    count, n_rows = len(ws), len(toks)
    shape = (2, groups, MOST, toks[0].shape[1] // 2)
    dma = pltpu.SemaphoreType.DMA
    return pl.pallas_call(
        functools.partial(gather_kernel, groups, count, n_rows),
        out_shape=[jax.ShapeDtypeStruct((4,) + w.shape, BF16) for w in ws]
        + [jax.ShapeDtypeStruct(shape, BF16)] * n_rows,
        in_specs=[VMEM] * (count + 2 * n_rows),
        out_specs=[HBM] * (count + n_rows),
        scratch_shapes=[
            pltpu.VMEM((n_rows,) + shape, BF16),
            dma((4 * count,)),
            dma((4 * count,)),
            dma((count,)),
            dma((n_rows, 2, groups)),
            dma((n_rows, 2, groups)),
            dma((n_rows,)),
        ],
        compiler_params=pltpu.CompilerParams(
            collective_id=0, has_side_effects=True, vmem_limit_bytes=24 * 2**20
        ),
    )(*ws, *picks, *toks)


def scatter_kernel(groups, *refs):
    row_in, out_grad, hidden, gate_grad, up_grad, w_gate, w_up, w_down = refs[:8]
    owns, from_x, from_y, backs = refs[8:11], refs[11:14], refs[14:17], refs[17:19]
    term, xs, far_x, far_y, sum_x, sum_y, others = refs[19:26]
    t_send, t_recv, x_send, x_recv, x_local, a_send, a_recv = refs[26:]
    at = Place(groups)
    block = term.shape[2]
    half = block // 2
    top, low = pl.ds(0, half), pl.ds(half, half)
    at.barrier(True)
    pending, first = [], []
    factors = ((out_grad, hidden), (row_in, gate_grad), (row_in, up_grad))
    rows = hidden.shape[0]
    swaps = [
        at.send(act, others.at[i], a_send, a_recv, i, at.pair)
        for i, (_, act) in enumerate(factors)
    ]

    def product(i, chip):
        a, b = factors[i]
        cols = pl.ds(pl.multiple_of(chip * block, block), block)
        own = dot(a[pl.ds(0, rows), cols], b[...], ((0,), (0,)))
        return (own + dot(a[pl.ds(rows, rows), cols], others[i], ((0,), (0,)))).astype(BF16)

    def send(i, n, src, dst, to):
        return at.send(src, dst, t_send, t_recv, 6 * i + n, to)

    for i in range(3):
        swaps[i].wait()
        term[i, 0] = product(i, at.chip_far)
        first.append(
            (
                send(i, 0, term.at[i, 0, top], far_x.at[i], at.to_x),
                send(i, 1, term.at[i, 0, low], far_y.at[i], at.to_y),
            )
        )
        term[i, 1] = product(i, at.chip_x)
        pending.append(send(i, 2, term.at[i, 1, top], from_x[i].at[top], at.to_x))
        term[i, 2] = product(i, at.chip_y)
        pending.append(send(i, 3, term.at[i, 2, low], from_y[i].at[low], at.to_y))
    turned = ((1,), (1,))
    for slot in range(2):
        act = others[0] if slot else hidden[...]
        xs[0, slot] = dot(act, w_down[...], turned).astype(BF16).reshape(xs.shape[2:])
    pending += at.rows(xs.at[0], backs[0], 0, x_send, x_recv, x_local)
    for slot in range(2):
        g, u = (others[1], others[2]) if slot else (gate_grad[...], up_grad[...])
        back = dot(g, w_gate[...], turned) + dot(u, w_up[...], turned)
        xs[1, slot] = back.astype(BF16).reshape(xs.shape[2:])
    pending += at.rows(xs.at[1], backs[1], 1, x_send, x_recv, x_local)
    for i in range(3):
        by_x, by_y = first[i]
        by_x.wait_recv()
        sum_y[i] = (term[i, 2, top].astype(F32) + far_x[i].astype(F32)).astype(BF16)
        pending.append(send(i, 4, sum_y.at[i], from_y[i].at[top], at.to_y))
        by_y.wait_recv()
        sum_x[i] = (term[i, 1, low].astype(F32) + far_y[i].astype(F32)).astype(BF16)
        pending.append(send(i, 5, sum_x.at[i], from_x[i].at[low], at.to_x))
        owns[i][...] = product(i, at.chip)
        by_x.wait_send()
        by_y.wait_send()
    for copy in pending:
        copy.wait()


def scatter_call(groups, block, row_in, out_grad, acts, ws):
    dma = pltpu.SemaphoreType.DMA
    ff = acts[0].shape[1]
    shape = (2, groups, MOST, row_in.shape[1])
    piece = pltpu.VMEM((3, block // 2, ff), BF16)
    return pl.pallas_call(
        functools.partial(scatter_kernel, groups),
        out_shape=[jax.ShapeDtypeStruct((block, ff), BF16)] * 9
        + [jax.ShapeDtypeStruct(shape, BF16)] * 2,
        in_specs=[VMEM] * 8,
        out_specs=[VMEM] * 3 + [HBM] * 8,
        scratch_shapes=[
            pltpu.VMEM((3, 3, block, ff), BF16),
            pltpu.VMEM((2,) + shape, BF16),
            piece,
            piece,
            piece,
            piece,
            pltpu.VMEM((3,) + acts[0].shape, BF16),
            dma((18,)),
            dma((18,)),
            dma((2, 2, groups)),
            dma((2, 2, groups)),
            dma((2,)),
            dma((3,)),
            dma((3,)),
        ],
        compiler_params=pltpu.CompilerParams(
            collective_id=1, has_side_effects=True, vmem_limit_bytes=48 * 2**20
        ),
    )(row_in, out_grad, *acts, *ws)


def routes(expert_ids, gate_vals, groups):
    per_index = EXPERTS // groups
    window = WAVE * groups
    tok_count = expert_ids.shape[0]
    local_index = expert_ids % per_index
    window_slot = jnp.where(
        local_index < WAVE, expert_ids // per_index * WAVE + local_index, window
    )
    slot_is = window_slot[:, :, None] == jnp.arange(window, dtype=jnp.int32)[None, None, :]
    chosen = jnp.any(slot_is, axis=1)
    gate_of = jnp.sum(jnp.where(slot_is, gate_vals.astype(F32)[:, :, None], 0.0), axis=1)
    tok = jnp.arange(tok_count, dtype=jnp.int32)
    before = (tok[:, None] > tok[None, :]).astype(BF16)
    rank = dot(before, chosen.astype(BF16), ((1,), (0,))).astype(jnp.int32)
    place = chosen[:, :, None] & (
        rank[:, :, None] == jnp.arange(MOST, dtype=jnp.int32)[None, None, :]
    )
    pick = place.astype(BF16).reshape(tok_count, window * MOST)
    weighted = (
        jnp.where(place, gate_of[:, :, None], 0.0).astype(BF16).reshape(tok_count, window * MOST)
    )
    return slot_is, place, pick, weighted


def on_device(tokens, expert_ids, gate_vals, w_gate, w_up, w_down, cotangent):
    groups = lax.axis_size("expert")
    columns = lax.axis_size("fsdp")
    side = lax.axis_index("fsdp") % 2
    tok_count, width = tokens.shape
    block = w_gate.shape[1]
    rows = groups * MOST
    sides = [[i for i in range(columns) if i % 2 == s] for s in (0, 1)]
    pairs = [(i, i ^ 1) for i in range(columns)]

    def swap(x):
        return lax.ppermute(x, "fsdp", pairs)

    def gather(w):
        return lax.all_gather(w[0], "fsdp", axis_index_groups=sides, axis=0, tiled=True)

    def scatter(x):
        return lax.psum_scatter(
            x.astype(BF16), "fsdp", scatter_dimension=0, axis_index_groups=sides, tiled=True
        ).astype(F32)[None]

    def cut(x, odd):
        return jnp.concatenate(
            [x[:, (2 * k + odd) * block : (2 * k + odd + 1) * block] for k in range(columns // 2)],
            axis=1,
        )

    def halves(x):
        even, odd = cut(x, 0), cut(x, 1)
        return jnp.where(side == 0, even, odd), jnp.where(side == 0, odd, even)

    def whole_rows(mine, other):
        even, odd = jnp.where(side == 0, mine, other), jnp.where(side == 0, other, mine)
        parts = []
        for k in range(columns // 2):
            here = slice(k * block, (k + 1) * block)
            parts += [even[:, here], odd[:, here]]
        return jnp.concatenate(parts, axis=1)

    def exchange(mine, other):
        packed = jnp.stack(
            [mine.reshape(groups, MOST, width // 2), other.reshape(groups, MOST, width // 2)],
            axis=1,
        )
        there = lax.all_to_all(packed, "expert", split_axis=0, concat_axis=0, tiled=True)
        return there[:, 0].reshape(rows, width // 2), there[:, 1].reshape(rows, width // 2)

    square = columns == 8
    slot_is, place, pick, weighted = routes(expert_ids, gate_vals, groups)
    first = ((0,), (0,))
    if square:
        *full, row_in, out_grad = gather_call(
            groups, [w_gate[0], w_up[0], w_down[0]], [pick, weighted], [tokens, cotangent]
        )
        full_gate, full_up, full_down = (w.reshape(width // 2, w.shape[2]) for w in full)
        row_in = row_in.reshape(2 * rows, width // 2)
        out_grad = out_grad.reshape(2 * rows, width // 2)
    else:
        full_gate, full_up, full_down = gather(w_gate), gather(w_up), gather(w_down)
        row_mine, row_other = exchange(*halves(dot(pick, tokens, first).astype(BF16)))
        og_mine, og_other = exchange(*halves(dot(weighted, cotangent, first).astype(BF16)))
        row_in = jnp.concatenate([row_mine, swap(row_other)], axis=0)
        out_grad = jnp.concatenate([og_mine, swap(og_other)], axis=0)

    def summed(x, w, dims):
        theirs = swap(dot(x[rows:], w, dims).astype(BF16))
        return dot(x[:rows], w, dims) + theirs.astype(F32)

    def both(x):
        return jnp.concatenate([x, swap(x)], axis=0)

    plain, turned = ((1,), (0,)), ((1,), (1,))
    gate_pre = summed(row_in, full_gate, plain)
    up_pre = summed(row_in, full_up, plain)
    sigmoid_g = jax.nn.sigmoid(gate_pre)
    hidden = (gate_pre * sigmoid_g * up_pre).astype(BF16)
    hidden_grad = summed(out_grad, full_down, plain)
    gate_grad = (
        hidden_grad * up_pre * sigmoid_g * (1.0 + gate_pre * (1.0 - sigmoid_g))
    ).astype(BF16)
    up_grad = (hidden_grad * gate_pre * sigmoid_g).astype(BF16)
    if square:
        got = scatter_call(
            groups,
            block,
            row_in,
            out_grad,
            [hidden, gate_grad, up_grad],
            [full_gate, full_up, full_down],
        )
        grad_w_down, grad_w_gate, grad_w_up = (
            (got[i].astype(F32) + got[3 + i].astype(F32) + got[6 + i].astype(F32))[None]
            for i in range(3)
        )
        outs, grads = ([r[i].reshape(rows, width // 2) for i in (0, 1)] for r in got[9:])
    else:
        hidden, gate_grad, up_grad = both(hidden), both(gate_grad), both(up_grad)
        grad_w_down = scatter(dot(out_grad, hidden, first))
        grad_w_gate = scatter(dot(row_in, gate_grad, first))
        grad_w_up = scatter(dot(row_in, up_grad, first))
        expert_out = dot(hidden, full_down, turned).astype(BF16)
        slot_grad = (
            dot(gate_grad, full_gate, turned) + dot(up_grad, full_up, turned)
        ).astype(BF16)
        outs = exchange(expert_out[:rows], swap(expert_out[rows:]))
        grads = exchange(slot_grad[:rows], swap(slot_grad[rows:]))

    slot_out = whole_rows(*outs)
    output = dot(weighted, slot_out, plain).astype(BF16)
    grad_tokens = dot(pick, whole_rows(*grads), plain).astype(BF16)
    met = dot(cotangent, slot_out, turned)
    met = jnp.sum(jnp.where(place, met.reshape(place.shape), 0.0), axis=2)
    grad_gates = jnp.sum(jnp.where(slot_is, met[:, None, :], 0.0), axis=2)
    return (output, grad_tokens, grad_gates, grad_w_gate, grad_w_up, grad_w_down)


def solution(mesh):
    token = P(("expert", "fsdp"), None)
    weight = P("expert", "fsdp", None)
    return jax.shard_map(
        on_device,
        mesh=mesh,
        in_specs=(token, token, token, weight, weight, weight, token),
        out_specs=(token, token, token, weight, weight, weight),
        check_vma=False,
    )
```
